256 devices in a mesh: bulk: 16 (over z, core), wide: 16 (over y, x).
Axes of the slice: x: 4, y: 4, z: 8, core: 2. Of those that a mesh axis runs over, the one named last changes fastest.
Arguments:
- wavefunction: float32 [16384, 512], P('wide'), may hold values from -6 to 6
- env_blocks: float32 [256, 2048, 1024], P('bulk', 'wide'), may hold values from -0.1875 to 0.1875
- right_env: float32 [32, 512, 512], P('bulk'), may hold values from -0.0625 to 0.0625
- tile_sector: int32 [128], replicated, may hold values from 0 to 31, never falling along the last dimension, each value on 1 to 8 neighbouring positions
- term_charge: int32 [32], replicated, may hold values from -1 to 1
- block_home: int32 [16, 16], replicated, may hold values from 0 to 15, as said below
Outputs:
- applied: float32 [16384, 512], P('wide', 'bulk')
The draws below stay inside these ranges and needn't reach their ends.
Inputs may be any that keep to these rules, and one draw needn't show every extreme that they name: `tile_sector`: never falls; each sector 0 to 31 covers 1 to 8 whole tiles, one exactly 8. `term_charge`: each MPO term raises, keeps or lowers the left quantum number by one. For each pair index k the column block_home[:, k] is a permutation of the bulk indices, so every device stores exactly one block of each k; at most 2 blocks of one term owner lie on one device, and some device holds 2 of them.
All inputs are finite; a program needn't handle non-finite values.
Results may differ from the reference program's by a relative error of at most 0.0003.
Values sent between devices are 32-bit elements; how exact they have to be, the bound alone decides.
No kernel may reach another device: no remote copies, remote signals or barrier semaphores. Data moves between devices by JAX's collectives and lax.ppermute only.
A program may use at most 192 MiB of HBM per device.

```python
import math
import jax
import jax.numpy as jnp
import numpy as np
from jax import lax

TILE = 128
MOST = 8
COLS = 512
NW_DEV = 2
TILE_DEV = 8
SRC = 1024
PAIRS = 16
TILES = 128
SECTORS = 32
NW = 32
HOMES = 16
N_WIDE = 16


def draw_block_home(key, part):
    subkeys = jax.random.split(key, 4)
    doubled = jax.random.randint(subkeys[0], (), 0, HOMES).astype(jnp.int32)
    others = jax.random.permutation(subkeys[1], 2 * HOMES - 2)[:PAIRS - 2].astype(jnp.int32)
    values = others // 2
    values = values + (values >= doubled).astype(jnp.int32)
    offsets = jnp.concatenate([jnp.stack([doubled, doubled]), values]).astype(jnp.int32)
    offsets = offsets[jax.random.permutation(subkeys[2], PAIRS)]
    relabel = jax.random.permutation(subkeys[3], HOMES).astype(jnp.int32)
    dest_rows = jnp.arange(HOMES, dtype=jnp.int32)
    return relabel[(dest_rows[:, None] + offsets[None, :]) % HOMES].astype(jnp.int32)


def plant(values, key, smallest, high):
    extent = values.shape
    spot = [jax.random.randint(jax.random.fold_in(key, axis), (), 0, extent[axis]) for axis in range(len(extent))]
    values = values.at[tuple(spot)].set(smallest)
    longest = extent.index(max(extent))
    spot[longest] = (spot[longest] + 1) % extent[longest]
    return values.at[tuple(spot)].set(high)


def spiked(result, key, source, target, shards_of, factor):
    def block_of(axis_at):
        return (jnp.arange(result.shape[axis_at]) // (result.shape[axis_at] // shards_of)).reshape((-1,) + (1,) * (result.ndim - 1 - axis_at))

    first = jax.random.permutation(key, shards_of)[block_of(target)]
    far = (block_of(target) + shards_of // 2) % shards_of
    return jnp.where((block_of(source) == first) | (block_of(source) == far), factor * result, result)


def block_scale(rng, shape, cuts, low, top_value):
    loudness, own = 1.0, jax.random.fold_in(rng, 6)
    for position, shards_of in cuts:
        steps = jnp.exp(jax.random.uniform(jax.random.fold_in(own, position), (shards_of,), jnp.float32, low / len(cuts), top_value / len(cuts)))
        loudness = loudness * jnp.repeat(steps, shape[position] // shards_of).reshape([-1 if axis == position else 1 for axis in range(len(shape))])
    return loudness


def split_up(amount, total, bound, slope):
    weights = [(1 << 20) // math.isqrt(grade ** slope) + 1 for grade in range(2, amount + 1)]
    surplus, holding = total - bound - (amount - 1), [1] * (amount - 1)
    while surplus > 0:
        free = [i for i in range(amount - 1) if holding[i] < bound]
        pool, budget = sum([weights[i] for i in free]), surplus
        for i in free:
            extra = min(bound - holding[i], max(1, budget * weights[i] // pool), surplus)
            holding[i] = holding[i] + extra
            surplus = surplus - extra
    return np.array([bound] + holding)


def uneven(key, amount, total, bound, slope):
    if amount == 2:
        one = jax.random.randint(key, (), max(1, total - bound), min(bound, total - 1) + 1)
        return jnp.stack([one, total - one])
    sizes = jnp.asarray(split_up(amount, total, bound, slope), jnp.int32)
    twos = (amount - 1) // 2
    donor, receiver = sizes[1:1 + 2 * twos:2], sizes[2:2 + 2 * twos:2]
    slack = jnp.minimum(donor - 1, bound - receiver)
    shifted = jax.random.randint(jax.random.fold_in(key, 1), (twos,), 0, 1 << 20) % (slack + 1)
    sizes = sizes.at[1:1 + 2 * twos:2].set(donor - shifted).at[2:2 + 2 * twos:2].set(receiver + shifted)
    return sizes[jax.random.permutation(jax.random.fold_in(key, 2), amount)]


def bell_draw(stream_key, dims, scale, limit, shards=(), kind=jnp.bfloat16):
    values = scale * jax.random.normal(stream_key, dims, jnp.float32)
    if shards:
        values = values * block_scale(stream_key, dims, shards, -0.22, 0.18)
    return jnp.clip(values, -limit, limit).astype(kind)


def bell_draw_with(rng, shape, deviation, reach, pieces, heavy, held_as=jnp.bfloat16):
    values = deviation * jax.random.normal(rng, shape, jnp.float32)
    if pieces:
        values = values * block_scale(rng, shape, pieces, -0.22, 0.18)
    return jnp.clip(spiked(values, jax.random.fold_in(rng, 3), *heavy), -reach, reach).astype(held_as)


def setup_inputs(seed: int = 0) -> dict:
    keys = jax.random.split(jax.random.key(seed), 7)
    return {
        "wavefunction": bell_draw(keys[0], (TILES * TILE, COLS), 1.0, 6.0, ((0, 16),), jnp.float32),
        "env_blocks": bell_draw(keys[1], (HOMES * PAIRS, N_WIDE * TILE, SRC), SRC ** -0.5, 0.1875, ((0, 16), (1, 16)), jnp.float32),
        "right_env": bell_draw_with(keys[2], (NW, COLS, COLS), (COLS * NW) ** -0.5, 0.0625, ((0, 16),), (0, 2, 16, 2.0), jnp.float32),
        "tile_sector": jnp.searchsorted(jnp.cumsum(uneven(keys[3], SECTORS, TILES, MOST, 2)), jnp.arange(TILES), side="right").astype(jnp.int32),
        "term_charge": plant(jax.random.randint(keys[4], (NW,), -1, 2), jax.random.fold_in(keys[4], 1), -1, 1).astype(jnp.int32),
        "block_home": draw_block_home(jax.random.fold_in(keys[6], 71), 0),
    }


precise = lax.Precision.HIGHEST


def reference(wavefunction, env_blocks, right_env, tile_sector, term_charge, block_home):
    labels = jnp.arange(TILES, dtype=jnp.int32)
    starts = jnp.sum((tile_sector[None, :] < labels[:, None]).astype(jnp.int32), axis=1)
    widths = jnp.sum((tile_sector[None, :] == labels[:, None]).astype(jnp.int32), axis=1)
    sectors = tile_sector[TILES - 1] + 1
    window_rows = jnp.arange(SRC, dtype=jnp.int32)
    padded = jnp.concatenate([wavefunction, jnp.zeros((SRC, COLS), wavefunction.dtype)], axis=0)

    def one_tile(tile_index):
        column = tile_index // TILE_DEV
        within = tile_index % TILE_DEV

        def add_term(term_index, total):
            term_index = jnp.asarray(term_index).astype(jnp.int32)
            holder = term_index // NW_DEV
            slot_index = within * NW_DEV + term_index % NW_DEV
            stored_at = block_home[holder, slot_index]
            source = tile_sector[tile_index] + term_charge[term_index]
            usable = (source >= 0) & (source < sectors)
            clipped = jnp.clip(source, 0, TILES - 1)
            live_rows = jnp.where(usable, widths[clipped] * TILE, 0)
            window = lax.dynamic_slice(padded, ((starts[clipped] * TILE).astype(jnp.int32), jnp.int32(0)), (SRC, COLS))
            window = jnp.where((window_rows < live_rows)[:, None], window, 0.0)
            env_block = lax.dynamic_slice(env_blocks, ((stored_at * PAIRS + slot_index).astype(jnp.int32), (column * TILE).astype(jnp.int32), jnp.int32(0)), (1, TILE, SRC))[0]
            left_part = jnp.dot(env_block, window, precision=precise, preferred_element_type=jnp.float32)
            return total + jnp.dot(left_part, right_env[term_index], precision=precise, preferred_element_type=jnp.float32)

        return lax.fori_loop(0, NW, add_term, jnp.zeros((TILE, COLS), jnp.float32))

    return lax.map(one_tile, labels).reshape(TILES * TILE, COLS)
```

```python
import jax
import jax.numpy as jnp
from jax import lax
from jax.experimental import pallas as pl
from jax.experimental.pallas import tpu as pltpu
from jax.sharding import PartitionSpec as P

TILE = 128
NW_DEV = 2
TILE_DEV = 8
SRC = 1024
PAIRS = 16
REACH = 2
COLS = 512
HOMES = 16
PART = COLS // HOMES
HALF = SRC // 2
SPAN = (2 * REACH + 1) * SRC


def from_behind(value, axis, steps):
    count = lax.axis_size(axis)
    initial, last = (max(0, -steps), min(count, count - steps))
    return lax.ppermute(value, axis, [(source, source + steps) for source in range(initial, last)])


def split(value):
    high = value.astype(jnp.bfloat16)
    return high, (value - high.astype(jnp.float32)).astype(jnp.bfloat16)


def dot(a, b):
    return jnp.dot(a, b, preferred_element_type=jnp.float32)


def window_plan(tile_sector, term_charge, tiles_of, terms_of):
    count_tiles = tile_sector.shape[0]
    labels = jnp.arange(count_tiles, dtype=jnp.int32)
    source = tile_sector[tiles_of] + term_charge[terms_of]
    sectors = tile_sector[count_tiles - 1] + 1
    usable = (source >= 0) & (source < sectors)
    clipped = jnp.clip(source, 0, count_tiles - 1)
    starts = jnp.sum((tile_sector[None, :] < clipped[:, None]).astype(jnp.int32), axis=1)
    widths = jnp.sum((tile_sector[None, :] == clipped[:, None]).astype(jnp.int32), axis=1)
    return starts, jnp.where(usable, widths * TILE, 0)


def left_kernel(plan, own, m0, m1, m2, m3, s0, s1, s2, s3, block, out, high, low):
    @pl.when(pl.program_id(0) == 0)
    def _():
        core = plan[2, 0]
        for spot, (mine, swapped) in zip((0, 1, 3, 4), ((m0, s0), (m1, s1), (m2, s2), (m3, s3))):
            for value, side in ((mine, core), (swapped, 1 - core)):
                rows = pl.ds(pl.multiple_of(spot * SRC + side * HALF, HALF), HALF)
                high[rows, :], low[rows, :] = split(value[...])
        rows = pl.ds(REACH * SRC, SRC)
        high[rows, :], low[rows, :] = split(own[...])

    k = pl.program_id(0)
    live = plan[1, k]
    rows = pl.ds(pl.multiple_of(plan[0, k] * TILE, TILE), SRC)
    columns = lax.broadcasted_iota(jnp.int32, (TILE, SRC), 1)
    b_high, b_low = split(jnp.where(columns < live, block[0], 0.0))
    both = dot(jnp.concatenate([b_high, b_low], axis=0), high[rows, :])
    left = both[:TILE] + both[TILE:] + dot(b_high, low[rows, :])
    out[...] = left.T.reshape(HOMES, 1, PART, TILE)


def left_products(plan, own, mine, swapped, blocks):
    whole = pl.BlockSpec((SRC, COLS), lambda k, plan: (0, 0))
    part = pl.BlockSpec((HALF, COLS), lambda k, plan: (0, 0))
    return pl.pallas_call(
        left_kernel,
        grid_spec=pltpu.PrefetchScalarGridSpec(
            num_scalar_prefetch=1,
            grid=(PAIRS,),
            in_specs=[whole] + [part] * 8 + [pl.BlockSpec((1, TILE, SRC), lambda k, plan: (k, 0, 0))],
            out_specs=pl.BlockSpec((HOMES, 1, PART, TILE), lambda k, plan: (0, k, 0, 0)),
            scratch_shapes=[pltpu.VMEM((SPAN, COLS), jnp.bfloat16), pltpu.VMEM((SPAN, COLS), jnp.bfloat16)],
        ),
        out_shape=jax.ShapeDtypeStruct((HOMES, PAIRS, PART, TILE), jnp.float32),
        name="left_products",
    )(plan, own, *mine, *swapped, blocks)


def right_kernel(home, parts, right, out, r_high, r_low, stack):
    tile = pl.program_id(0)

    @pl.when(tile == 0)
    def _():
        r_high[...], r_low[...] = split(right[...].T)

    for w in range(HOMES * NW_DEV):
        k = tile * NW_DEV + w % NW_DEV
        stack[w * PART:(w + 1) * PART, :] = parts[home[w // NW_DEV, k], k]
    high, low = split(stack[...])
    total = dot(r_high[...], high) + dot(r_low[...], high) + dot(r_high[...], low)
    out[...] = total


def right_products(home, parts, right):
    depth = HOMES * NW_DEV * PART
    return pl.pallas_call(
        right_kernel,
        grid_spec=pltpu.PrefetchScalarGridSpec(
            num_scalar_prefetch=1,
            grid=(TILE_DEV,),
            in_specs=[
                pl.BlockSpec((HOMES, PAIRS, PART, TILE), lambda t, home: (0, 0, 0, 0)),
                pl.BlockSpec((depth, COLS), lambda t, home: (0, 0)),
            ],
            out_specs=pl.BlockSpec((COLS, TILE), lambda t, home: (0, t)),
            scratch_shapes=[
                pltpu.VMEM((COLS, depth), jnp.bfloat16),
                pltpu.VMEM((COLS, depth), jnp.bfloat16),
                pltpu.VMEM((depth, TILE), jnp.float32),
            ],
        ),
        out_shape=jax.ShapeDtypeStruct((COLS, TILE_DEV * TILE), jnp.float32),
        name="right_products",
    )(home, parts, right)


def exchange(value):
    return lax.all_to_all(value, "bulk", split_axis=0, concat_axis=0, tiled=True)


def on_device(wavefunction, env_blocks, right_env, tile_sector, term_charge, block_home):
    here = lax.axis_index("bulk")
    column = lax.axis_index("wide")
    core = here % 2
    right = exchange(right_env.reshape(NW_DEV, HOMES, PART, COLS).transpose(1, 0, 2, 3))
    right = right.reshape(HOMES * NW_DEV * PART, COLS)

    half = lax.dynamic_slice(wavefunction, (core * HALF, jnp.int32(0)), (HALF, COLS))
    mine = [from_behind(half, "wide", offset) for offset in (2, 1, -1, -2)]
    pairs = [(index, index ^ 1) for index in range(HOMES)]
    swapped = [lax.ppermute(value, "bulk", pairs) for value in mine]

    pair_ids = jnp.arange(PAIRS, dtype=jnp.int32)
    homes = jnp.arange(HOMES, dtype=jnp.int32)
    owner = jnp.sum(homes[:, None] * (block_home == here).astype(jnp.int32), axis=0)
    first_tile, live_rows = window_plan(
        tile_sector, term_charge, column * TILE_DEV + pair_ids // NW_DEV, owner * NW_DEV + pair_ids % NW_DEV
    )
    first = jnp.clip(first_tile - (column - REACH) * TILE_DEV, 0, SPAN // TILE - TILE_DEV)
    plan = jnp.stack([first, live_rows, jnp.full((PAIRS,), core, jnp.int32)])

    parts = exchange(left_products(plan, wavefunction, mine, swapped, env_blocks))
    partial = right_products(block_home, parts, right)
    pieces = exchange(partial.reshape(HOMES, PART, TILE_DEV * TILE))
    return jnp.sum(pieces, axis=0).T


def solution(mesh):
    return jax.shard_map(
        on_device,
        mesh=mesh,
        in_specs=(P("wide", None), P("bulk", "wide", None), P("bulk", None, None), P(), P(), P()),
        out_specs=P("wide", "bulk"),
        check_vma=False,
    )
```
